32 devices in a mesh: row: 8 (over y, x, core), col: 4 (over z).
Axes of the slice: x: 2, y: 2, z: 4, core: 2. Of those that a mesh axis runs over, the one named last changes fastest.
Arguments:
- final_amp: bfloat16 [8, 32, 128, 440], P('row', 'col'), may hold values from -0.19921875 to 0.19921875
- initial_amp: bfloat16 [4, 32, 128, 440], P('col', 'row'), may hold values from -0.19921875 to 0.19921875
- pair_final: int32 [8, 4, 128], P('row', 'col'), may hold values from 0 to 31
- pair_initial: int32 [8, 4, 128], P('row', 'col'), may hold values from 0 to 31
- map_final: int32 [8, 32, 440], P('row', 'col'), may hold values from 0 to 439, each once within a row
- map_initial: int32 [4, 32, 440], P('col', 'row'), may hold values from 0 to 439, each once within a row
- counts: int32 [8, 4], P('row', 'col'), may hold values from 16 to 128, as said below
Outputs:
- density: float32 [440, 440], replicated
The draws below stay inside these ranges and needn't reach their ends.
Inputs may be any that keep to these rules, and one draw needn't show every extreme that they name: `counts`: slots at or past a cell's count are ignored. Exactly one cell of every draw has 128 live slots.
All inputs are finite; a program needn't handle non-finite values.
Results may differ from the reference program's by a relative error of at most 0.0003.
Values may be sent and summed in bfloat16 or wider, within the bound.
A program may use at most 64 MiB of HBM per device.

```python
import jax
import jax.numpy as jnp
from jax import lax

ORB = 440
BLK = 128
SEGB = 32
K = 128
GROUP = 32
GRID_ROWS = 8
GRID_COLS = 4


def draw_counts(key, part):
    base_key, busy_key = jax.random.split(jax.random.fold_in(key, 11))
    base = jax.random.randint(base_key, (GRID_ROWS, GRID_COLS), K // 8, K // 2 + 1, dtype=jnp.int32)
    busiest = jax.random.randint(busy_key, (), 0, GRID_ROWS * GRID_COLS, dtype=jnp.int32)
    cells = jnp.arange(GRID_ROWS * GRID_COLS, dtype=jnp.int32).reshape(GRID_ROWS, GRID_COLS)
    return jnp.where(cells == busiest, K, base).astype(jnp.int32)


def plant(entries, key, smallest, top_value):
    place = [jax.random.randint(jax.random.fold_in(key, axis), (), 0, length) for axis, length in enumerate(entries.shape)]
    widest = entries.shape.index(max(entries.shape))
    next_to = place[:widest] + [(place[widest] + 1) % entries.shape[widest]] + place[widest + 1:]
    return entries.at[tuple(place)].set(smallest).at[tuple(next_to)].set(top_value)


def shard_levels(rng, extent, pieces, smallest, top_value):
    def one(dim, blocks):
        steps = jax.random.uniform(jax.random.fold_in(jax.random.fold_in(rng, 6), dim), (blocks,), jnp.float32, smallest / len(pieces), top_value / len(pieces))
        return jnp.repeat(jnp.exp(steps), extent[dim] // blocks).reshape((-1,) + (1,) * (len(extent) - dim - 1))

    loudness = one(*pieces[0])
    for cut in pieces[1:]:
        loudness = loudness * one(*cut)
    return loudness


def centred(rng, dims, scale, reach, cuts=(), kind=jnp.bfloat16):
    level = shard_levels(rng, dims, cuts, -0.22, 0.18) if cuts else 1.0
    array = jax.random.normal(rng, dims, jnp.float32) * scale * level
    return jnp.minimum(jnp.maximum(array, -reach), reach).astype(kind)


def setup_inputs(seed: int = 0) -> dict:
    splits = jax.random.split(jax.random.key(seed), 8)
    return {
        "final_amp": centred(splits[0], (GRID_ROWS, SEGB, BLK, ORB), 0.03, 0.19921875, ((0, 8), (1, 4))),
        "initial_amp": centred(splits[1], (GRID_COLS, SEGB, BLK, ORB), 0.03, 0.19921875, ((0, 4), (1, 8))),
        "pair_final": plant(jax.random.randint(splits[2], (GRID_ROWS, GRID_COLS, K), 0, SEGB), jax.random.fold_in(splits[2], 1), 0, SEGB - 1).astype(jnp.int32),
        "pair_initial": plant(jax.random.randint(splits[3], (GRID_ROWS, GRID_COLS, K), 0, SEGB), jax.random.fold_in(splits[3], 1), 0, SEGB - 1).astype(jnp.int32),
        "map_final": jax.vmap(lambda own: jax.random.permutation(own, ORB))(jax.random.split(splits[4], GRID_ROWS * SEGB)).reshape((GRID_ROWS, SEGB, ORB)).astype(jnp.int32),
        "map_initial": jax.vmap(lambda own: jax.random.permutation(own, ORB))(jax.random.split(splits[5], GRID_COLS * SEGB)).reshape((GRID_COLS, SEGB, ORB)).astype(jnp.int32),
        "counts": draw_counts(jax.random.fold_in(splits[7], 71), 0),
    }


def permute_columns(blocks, orbital_map):
    return jnp.take(blocks, orbital_map, axis=1)


def cell_density(final_seg, initial_seg, slots_final, slots_initial, live_count):
    def advance(index, summed):
        first_slot = index * GROUP
        which_final = lax.dynamic_slice_in_dim(slots_final, first_slot, GROUP)
        which_initial = lax.dynamic_slice_in_dim(slots_initial, first_slot, GROUP)
        live_mask = (first_slot + jnp.arange(GROUP, dtype=jnp.int32)) < live_count
        left = jnp.take(final_seg, which_final, axis=0)
        right = jnp.take(initial_seg, which_initial, axis=0)
        left = jnp.where(live_mask[:, None, None], left, jnp.zeros_like(left))
        return summed + jnp.dot(left.reshape(-1, ORB).T, right.reshape(-1, ORB), preferred_element_type=jnp.float32)

    turns = (live_count + GROUP - 1) // GROUP
    return lax.fori_loop(0, turns, advance, jnp.zeros((ORB, ORB), jnp.float32))


def reference(final_amp, initial_amp, pair_final, pair_initial, map_final, map_initial, counts):
    def add_cell(cell, summed):
        brow = cell // GRID_COLS
        bcol = cell % GRID_COLS
        final_seg = lax.dynamic_index_in_dim(final_amp, brow, 0, keepdims=False)
        initial_seg = lax.dynamic_index_in_dim(initial_amp, bcol, 0, keepdims=False)
        fmap = lax.dynamic_index_in_dim(map_final, brow, 0, keepdims=False)
        imap = lax.dynamic_index_in_dim(map_initial, bcol, 0, keepdims=False)
        final_seg = jax.vmap(permute_columns)(final_seg, fmap)
        initial_seg = jax.vmap(permute_columns)(initial_seg, imap)
        return summed + cell_density(final_seg, initial_seg, pair_final[brow, bcol], pair_initial[brow, bcol], counts[brow, bcol])

    return lax.fori_loop(0, GRID_ROWS * GRID_COLS, add_cell, jnp.zeros((ORB, ORB), jnp.float32))
```

```python
import functools

import jax
import jax.numpy as jnp
from jax import lax
from jax.experimental import pallas as pl
from jax.experimental.pallas import tpu as pltpu
from jax.sharding import PartitionSpec as P

MESH = pl.DeviceIdType.MESH
UNROLL = 4


def flip(value, bit):
    return value + bit - 2 * bit * lax.rem(lax.div(value, bit), 2)


def flip_many(value, mask):
    bit = 1
    while bit <= mask:
        if mask & bit:
            value = flip(value, bit)
        bit *= 2
    return value


def relay_plan(rows):
    bits = []
    bit = 2
    while bit < rows:
        bits.append(bit)
        bit *= 2
    plans = []
    for order in (bits, bits[::-1]):
        diffs = [(0, 0)]
        for position, bit in enumerate(order):
            diffs += [(diff | bit, position + 1) for diff, _ in list(diffs)]
        plans.append((order, diffs))
    return plans


def permute(block, orbital_map):
    orbitals = block.shape[1]
    chosen = lax.broadcasted_iota(jnp.int32, (orbitals, orbitals), 0) == orbital_map
    onehot = jnp.where(chosen, 1.0, 0.0).astype(jnp.bfloat16)
    moved = jnp.dot(block, onehot, preferred_element_type=jnp.float32)
    return moved.T.astype(jnp.bfloat16)


def spread_kernel(rows, cols, fin_ref, ini_ref, fmap_ref, imap_ref, list_ref, f_all, i_all, l_all,
                  f_own, i_own, zero, local_sem, send_sem, recv_sem, zsend, zrecv, fsend, frecv, lsend, lrecv):
    r = lax.axis_index("row")
    c = lax.axis_index("col")
    groups = cols // 2
    own_i = ini_ref.shape[0]
    own_f = fin_ref.shape[0]
    half = own_i // 2
    plans = relay_plan(rows)

    barrier = pltpu.get_barrier_semaphore()
    peers = []
    bit = 1
    while bit < rows:
        peers.append((flip(r, bit), c))
        bit *= 2
    peers += [(r, flip_many(c, mask)) for mask in [1] + [2 * g for g in range(1, groups)]]
    for peer in peers:
        pl.semaphore_signal(barrier, inc=1, device_id=peer, device_id_type=MESH)

    for j in range(own_i):
        i_own[j] = permute(ini_ref[j], imap_ref[j])
    pl.semaphore_wait(barrier, len(peers))

    sent = []

    def remote(src, dst, ssem, rsem, peer):
        copy = pltpu.make_async_remote_copy(src_ref=src, dst_ref=dst, send_sem=ssem, recv_sem=rsem,
                                            device_id=peer, device_id_type=MESH)
        copy.start()
        sent.append(copy)

    def part(h):
        return pl.ds(h * half, half)

    used = {}

    def forward(g, h, diff, position, src):
        order, _ = plans[h]
        targets = order[position:] + [1]
        for bit in targets:
            k = used.setdefault((g, h), 0)
            used[(g, h)] = k + 1
            remote(src, i_all.at[g, diff ^ bit, part(h)], send_sem.at[g, h, k], recv_sem.at[g, h, diff ^ bit],
                   (flip(r, bit), c))

    for h in range(2):
        for g in range(1, groups):
            remote(i_own.at[part(h)], i_all.at[g, 0, part(h)], zsend.at[g, h], zrecv.at[g, h], (r, flip_many(c, 2 * g)))
        forward(0, h, 0, 0, i_own.at[part(h)])
    for g in range(1, groups):
        remote(list_ref, l_all.at[g], lsend.at[g], lrecv.at[g], (r, flip_many(c, 2 * g)))

    local = [pltpu.make_async_copy(i_own, i_all.at[0, 0], local_sem.at[0]),
             pltpu.make_async_copy(list_ref, l_all.at[0], local_sem.at[1])]
    zero[...] = jnp.zeros_like(zero)
    for j in range(own_f):
        f_own[j] = permute(fin_ref[j], fmap_ref[j])
    remote(f_own, f_all.at[pl.ds(own_f, own_f)], fsend, frecv, (r, flip(c, 1)))
    local += [pltpu.make_async_copy(f_own, f_all.at[pl.ds(0, own_f)], local_sem.at[2]),
              pltpu.make_async_copy(zero, f_all.at[2 * own_f], local_sem.at[3])]
    for copy in local:
        copy.start()

    def arrived(ref, ssem, rsem):
        pltpu.make_async_remote_copy(src_ref=ref, dst_ref=ref, send_sem=ssem, recv_sem=rsem,
                                     device_id=(flip(r, 1), c), device_id_type=MESH).wait_recv()

    def relay(g, h, diff, position):
        here = i_all.at[g, diff, part(h)]
        if diff == 0:
            arrived(here, zsend.at[g, h], zrecv.at[g, h])
        else:
            arrived(here, send_sem.at[g, h, 0], recv_sem.at[g, h, diff])
        forward(g, h, diff, position, here)

    longest = len(plans[0][1])
    for wave in range(groups + longest):
        for g in range(groups):
            index = wave - g + 1
            if g == 0 and index == 0:
                continue
            for h in range(2):
                if g > 0:
                    index = wave - g
                if 0 <= index < longest:
                    diff, position = plans[h][1][index]
                    if g == 0 and diff == 0:
                        continue
                    relay(g, h, diff, position)
    for g in range(groups):
        for h in range(2):
            for diff, _ in plans[h][1]:
                arrived(i_all.at[g, diff ^ 1, part(h)], send_sem.at[g, h, 0], recv_sem.at[g, h, diff ^ 1])
    for g in range(1, groups):
        arrived(l_all.at[g], lsend.at[g], lrecv.at[g])
    arrived(f_all.at[pl.ds(own_f, own_f)], fsend, frecv)
    for copy in sent:
        copy.wait_send()
    for copy in local:
        copy.wait()


def density_kernel(rows, cols, own_f, own_i, f_ref, i_ref, l_ref, out_ref, list_f, list_i):
    r = lax.axis_index("row")
    c = lax.axis_index("col")
    groups = cols // 2
    total = jnp.int32(0)
    for g in range(groups):
        def collect(p, n):
            q = l_ref[g, 0, p]
            s = l_ref[g, 1, p]
            apart = lax.div(q, own_f) ^ c
            list_f[n] = apart * own_f + lax.rem(q, own_f)
            list_i[n] = (g * rows + (lax.div(s, own_i) ^ r)) * own_i + lax.rem(s, own_i)
            return n + jnp.where(apart < 2, 1, 0).astype(jnp.int32)

        total = lax.fori_loop(0, l_ref[g, 2, 0], collect, total)
    for k in range(UNROLL):
        list_f[total + k] = 2 * own_f
        list_i[total + k] = 0
    out_ref[...] = jnp.zeros_like(out_ref)

    def step(t, carry):
        first = t * UNROLL
        left = jnp.concatenate([f_ref[list_f[first + k]] for k in range(UNROLL)], axis=1)
        right = jnp.concatenate([i_ref[list_i[first + k]] for k in range(UNROLL)], axis=1)
        out_ref[...] += lax.dot_general(left, right, (((1,), (1,)), ((), ())), preferred_element_type=jnp.float32)
        return carry

    lax.fori_loop(0, lax.div(total + UNROLL - 1, UNROLL), step, 0)


def shards(rows, cols, final_amp, initial_amp, pair_final, pair_initial, map_final, map_initial, counts):
    own_f, blk, orb = final_amp.shape[1:]
    own_i = initial_amp.shape[1]
    slots = pair_final.shape[2]
    groups = cols // 2
    lists = jnp.concatenate([pair_final[0], pair_initial[0], jnp.broadcast_to(counts, (6, slots))], axis=0)
    vmem = pl.BlockSpec(memory_space=pltpu.VMEM)
    hbm = pl.BlockSpec(memory_space=pl.ANY)
    dma = pltpu.SemaphoreType.DMA
    f_all, i_all, l_all = pl.pallas_call(
        functools.partial(spread_kernel, rows, cols),
        out_shape=(jax.ShapeDtypeStruct((2 * own_f + 1, orb, blk), jnp.bfloat16),
                   jax.ShapeDtypeStruct((groups, rows, own_i, orb, blk), jnp.bfloat16),
                   jax.ShapeDtypeStruct((groups, 8, slots), jnp.int32)),
        in_specs=[vmem] * 5,
        out_specs=(hbm, hbm, hbm),
        scratch_shapes=[pltpu.VMEM((own_f, orb, blk), jnp.bfloat16), pltpu.VMEM((own_i, orb, blk), jnp.bfloat16),
                        pltpu.VMEM((orb, blk), jnp.bfloat16),
                        dma((4,)), dma((groups, 2, rows)), dma((groups, 2, rows)),
                        dma((groups, 2)), dma((groups, 2)), dma, dma, dma((groups,)), dma((groups,))],
        compiler_params=pltpu.CompilerParams(collective_id=0, has_side_effects=True, vmem_limit_bytes=40 << 20),
    )(final_amp[0], initial_amp[0], map_final[0][:, None], map_initial[0][:, None], lists)
    i_all = i_all.reshape(-1, orb, blk)
    partial = pl.pallas_call(
        functools.partial(density_kernel, rows, cols, own_f, own_i),
        out_shape=jax.ShapeDtypeStruct((orb, orb), jnp.float32),
        in_specs=[vmem, vmem, pl.BlockSpec(memory_space=pltpu.SMEM)],
        out_specs=vmem,
        scratch_shapes=[pltpu.SMEM((groups * slots + UNROLL,), jnp.int32)] * 2,
        compiler_params=pltpu.CompilerParams(vmem_limit_bytes=50 << 20),
    )(f_all, i_all, l_all)
    band = lax.psum_scatter(partial, "col", scatter_dimension=0, tiled=True)
    band = lax.psum(band, "row")
    return lax.all_gather(band, "col", axis=0, tiled=True)


def solution(mesh):
    placed = (
        P("row", "col", None, None),
        P("col", "row", None, None),
        P("row", "col", None),
        P("row", "col", None),
        P("row", "col", None),
        P("col", "row", None),
        P("row", "col"),
    )
    body = functools.partial(shards, mesh.shape["row"], mesh.shape["col"])
    return jax.shard_map(body, mesh=mesh, in_specs=placed, out_specs=P(), check_vma=False)
```

```python
import functools

import jax
import jax.numpy as jnp
from jax import lax
from jax.experimental import pallas as pl
from jax.experimental.pallas import tpu as pltpu
from jax.sharding import PartitionSpec as P

MESH = pl.DeviceIdType.MESH
UNROLL = 4
LANES = 128


def flip(value, bit):
    return value + bit - 2 * bit * lax.rem(lax.div(value, bit), 2)


def flip_many(value, mask):
    bit = 1
    while bit <= mask:
        if mask & bit:
            value = flip(value, bit)
        bit *= 2
    return value


def relay_plan(rows):
    bits = []
    bit = 2
    while bit < rows:
        bits.append(bit)
        bit *= 2
    plans = []
    for order in (bits, bits[::-1]):
        diffs = [(0, 0)]
        for position, bit in enumerate(order):
            diffs += [(diff | bit, position + 1) for diff, _ in list(diffs)]
        plans.append((order, diffs))
    return plans


def permute(block, orbital_map):
    orbitals = block.shape[1]
    chosen = lax.broadcasted_iota(jnp.int32, (orbitals, orbitals), 0) == orbital_map
    onehot = jnp.where(chosen, 1.0, 0.0).astype(jnp.bfloat16)
    moved = jnp.dot(block, onehot, preferred_element_type=jnp.float32)
    return moved.T.astype(jnp.bfloat16)


def spread_kernel(rows, cols, fin_ref, ini_ref, fmap_ref, imap_ref, list_ref, f_all, i_all, l_all,
                  f_own, i_own, zero, local_sem, send_sem, recv_sem, zsend, zrecv, fsend, frecv, lsend, lrecv):
    r = lax.axis_index("row")
    c = lax.axis_index("col")
    groups = cols // 2
    own_i = ini_ref.shape[0]
    own_f = fin_ref.shape[0]
    half = own_i // 2
    plans = relay_plan(rows)

    barrier = pltpu.get_barrier_semaphore()
    peers = []
    bit = 1
    while bit < rows:
        peers.append((flip(r, bit), c))
        bit *= 2
    peers += [(r, flip_many(c, mask)) for mask in [1] + [2 * g for g in range(1, groups)]]
    for peer in peers:
        pl.semaphore_signal(barrier, inc=1, device_id=peer, device_id_type=MESH)

    for j in range(own_i):
        i_own[j] = permute(ini_ref[j], imap_ref[j])
    pl.semaphore_wait(barrier, len(peers))

    sent = []

    def remote(src, dst, ssem, rsem, peer):
        copy = pltpu.make_async_remote_copy(src_ref=src, dst_ref=dst, send_sem=ssem, recv_sem=rsem,
                                            device_id=peer, device_id_type=MESH)
        copy.start()
        sent.append(copy)

    def part(h):
        return pl.ds(h * half, half)

    used = {}

    def forward(g, h, diff, position, src):
        order, _ = plans[h]
        targets = order[position:] + [1]
        for bit in targets:
            k = used.setdefault((g, h), 0)
            used[(g, h)] = k + 1
            remote(src, i_all.at[g, diff ^ bit, part(h)], send_sem.at[g, h, k], recv_sem.at[g, h, diff ^ bit],
                   (flip(r, bit), c))

    for h in range(2):
        for g in range(1, groups):
            remote(i_own.at[part(h)], i_all.at[g, 0, part(h)], zsend.at[g, h], zrecv.at[g, h], (r, flip_many(c, 2 * g)))
        forward(0, h, 0, 0, i_own.at[part(h)])
    for g in range(1, groups):
        remote(list_ref, l_all.at[g], lsend.at[g], lrecv.at[g], (r, flip_many(c, 2 * g)))

    local = [pltpu.make_async_copy(i_own, i_all.at[0, 0], local_sem.at[0]),
             pltpu.make_async_copy(list_ref, l_all.at[0], local_sem.at[1])]
    zero[...] = jnp.zeros_like(zero)
    for j in range(own_f):
        f_own[j] = permute(fin_ref[j], fmap_ref[j])
    remote(f_own, f_all.at[pl.ds(own_f, own_f)], fsend, frecv, (r, flip(c, 1)))
    local += [pltpu.make_async_copy(f_own, f_all.at[pl.ds(0, own_f)], local_sem.at[2]),
              pltpu.make_async_copy(zero, f_all.at[2 * own_f], local_sem.at[3])]
    for copy in local:
        copy.start()

    def arrived(ref, ssem, rsem):
        pltpu.make_async_remote_copy(src_ref=ref, dst_ref=ref, send_sem=ssem, recv_sem=rsem,
                                     device_id=(flip(r, 1), c), device_id_type=MESH).wait_recv()

    def relay(g, h, diff, position):
        here = i_all.at[g, diff, part(h)]
        if diff == 0:
            arrived(here, zsend.at[g, h], zrecv.at[g, h])
        else:
            arrived(here, send_sem.at[g, h, 0], recv_sem.at[g, h, diff])
        forward(g, h, diff, position, here)

    longest = len(plans[0][1])
    for wave in range(groups + longest):
        for g in range(groups):
            index = wave - g + 1
            if g == 0 and index == 0:
                continue
            for h in range(2):
                if g > 0:
                    index = wave - g
                if 0 <= index < longest:
                    diff, position = plans[h][1][index]
                    if g == 0 and diff == 0:
                        continue
                    relay(g, h, diff, position)
    for g in range(groups):
        for h in range(2):
            for diff, _ in plans[h][1]:
                arrived(i_all.at[g, diff ^ 1, part(h)], send_sem.at[g, h, 0], recv_sem.at[g, h, diff ^ 1])
    for g in range(1, groups):
        arrived(l_all.at[g], lsend.at[g], lrecv.at[g])
    arrived(f_all.at[pl.ds(own_f, own_f)], fsend, frecv)
    for copy in sent:
        copy.wait_send()
    for copy in local:
        copy.wait()


def density_kernel(rows, cols, own_f, own_i, f_ref, i_ref, l_ref, out_ref, acc, list_f, list_i):
    r = lax.axis_index("row")
    c = lax.axis_index("col")
    groups = cols // 2
    total = jnp.int32(0)
    for g in range(groups):
        def collect(p, n):
            q = l_ref[g, 0, p]
            s = l_ref[g, 1, p]
            apart = lax.div(q, own_f) ^ c
            list_f[n] = apart * own_f + lax.rem(q, own_f)
            list_i[n] = (g * rows + (lax.div(s, own_i) ^ r)) * own_i + lax.rem(s, own_i)
            return n + jnp.where(apart < 2, 1, 0).astype(jnp.int32)

        total = lax.fori_loop(0, l_ref[g, 2, 0], collect, total)
    for k in range(UNROLL):
        list_f[total + k] = 2 * own_f
        list_i[total + k] = 0
    acc[...] = jnp.zeros_like(acc)

    def step(t, carry):
        first = t * UNROLL
        left = jnp.concatenate([f_ref[list_f[first + k]] for k in range(UNROLL)], axis=1)
        right = jnp.concatenate([i_ref[list_i[first + k]] for k in range(UNROLL)], axis=1)
        acc[...] += lax.dot_general(left, right, (((1,), (1,)), ((), ())), preferred_element_type=jnp.float32)
        return carry

    lax.fori_loop(0, lax.div(total + UNROLL - 1, UNROLL), step, 0)
    orb = acc.shape[0]
    for block, first in enumerate(range(0, orb, LANES)):
        width = min(LANES, orb - first)
        if width < LANES:
            out_ref[block * orb:, :] = jnp.zeros((out_ref.shape[0] - block * orb, LANES), jnp.float32)
        out_ref[block * orb:(block + 1) * orb, :width] = acc[:, first:first + width]
    tail = pl.cdiv(orb, LANES) * orb
    if tail < out_ref.shape[0]:
        out_ref[tail:, :] = jnp.zeros((out_ref.shape[0] - tail, LANES), jnp.float32)


def reduce_kernel(rows, cols, part_ref, out_ref, acc, res, rbuf, zbuf,
                  rs_send, rs_recv, z_send, z_recv, g_send, g_recv, ag_send, ag_recv):
    r = lax.axis_index("row")
    c = lax.axis_index("col")
    half = part_ref.shape[0] // 2
    orders = [[1] + order for order, _ in relay_plan(rows)]
    steps = len(orders[0])

    barrier = pltpu.get_barrier_semaphore()
    peers = [(flip(r, bit), c) for bit in orders[0]] + [(r, flip_many(c, mask)) for mask in range(1, cols)]
    for peer in peers:
        pl.semaphore_signal(barrier, inc=1, device_id=peer, device_id_type=MESH)
    pl.semaphore_wait(barrier, len(peers))

    sent = []

    def remote(src, dst, ssem, rsem, peer):
        copy = pltpu.make_async_remote_copy(src_ref=src, dst_ref=dst, send_sem=ssem, recv_sem=rsem,
                                            device_id=peer, device_id_type=MESH)
        copy.start()
        sent.append(copy)
        return copy

    def rows_at(first, size):
        return pl.ds(pl.multiple_of(first, 8), size)

    start = [r * 0, r * 0 + half]
    size = half
    used = 0
    for step in range(steps):
        size //= 2
        source = part_ref if step == 0 else acc
        copies = []
        for h in range(2):
            bit = orders[h][step]
            mine = lax.rem(lax.div(r, bit), 2)
            give = start[h] + (1 - mine) * size
            start[h] = start[h] + mine * size
            copies.append(remote(source.at[rows_at(give, size)], rbuf.at[h, pl.ds(used, size)],
                                 rs_send.at[h, step], rs_recv.at[h, step], (flip(r, bit), c)))
        for h in range(2):
            copies[h].wait_recv()
            keep = rows_at(start[h], size)
            acc[keep, :] = source[keep, :] + rbuf[h, used:used + size, :]
        used += size

    share = cols // 2
    sub = size // share

    def band(k):
        return rows_at(start[0] + (start[1] - start[0]) * lax.div(k, share) + lax.rem(k, share) * sub, sub)

    own = band(c)
    copies = []
    for mask in range(1, cols):
        peer = flip_many(c, mask)
        copies.append(remote(acc.at[band(peer)], zbuf.at[mask - 1], z_send.at[mask], z_recv.at[mask], (r, peer)))
    value = acc[own, :]
    for mask in range(1, cols):
        copies[mask - 1].wait_recv()
        value = value + zbuf[mask - 1]
    res[own, :] = value
    copies = []
    for mask in range(1, cols):
        copies.append(remote(res.at[own], res.at[own], g_send.at[mask], g_recv.at[mask], (r, flip_many(c, mask))))
    for copy in copies:
        copy.wait_recv()
    for step in reversed(range(steps)):
        copies = []
        for h in range(2):
            bit = orders[h][step]
            here = res.at[rows_at(start[h], size)]
            copies.append(remote(here, here, ag_send.at[h, step], ag_recv.at[h, step], (flip(r, bit), c)))
        for h in range(2):
            copies[h].wait_recv()
            start[h] = start[h] - lax.rem(lax.div(r, orders[h][step]), 2) * size
        size *= 2
    orb = out_ref.shape[0]
    for block, first in enumerate(range(0, orb, LANES)):
        width = min(LANES, orb - first)
        out_ref[:, first:first + width] = res[block * orb:(block + 1) * orb, :width]
    for copy in sent:
        copy.wait_send()


def shards(rows, cols, final_amp, initial_amp, pair_final, pair_initial, map_final, map_initial, counts):
    own_f, blk, orb = final_amp.shape[1:]
    own_i = initial_amp.shape[1]
    slots = pair_final.shape[2]
    groups = cols // 2
    lists = jnp.concatenate([pair_final[0], pair_initial[0], jnp.broadcast_to(counts, (6, slots))], axis=0)
    vmem = pl.BlockSpec(memory_space=pltpu.VMEM)
    hbm = pl.BlockSpec(memory_space=pl.ANY)
    dma = pltpu.SemaphoreType.DMA
    f_all, i_all, l_all = pl.pallas_call(
        functools.partial(spread_kernel, rows, cols),
        out_shape=(jax.ShapeDtypeStruct((2 * own_f + 1, orb, blk), jnp.bfloat16),
                   jax.ShapeDtypeStruct((groups, rows, own_i, orb, blk), jnp.bfloat16),
                   jax.ShapeDtypeStruct((groups, 8, slots), jnp.int32)),
        in_specs=[vmem] * 5,
        out_specs=(hbm, hbm, hbm),
        scratch_shapes=[pltpu.VMEM((own_f, orb, blk), jnp.bfloat16), pltpu.VMEM((own_i, orb, blk), jnp.bfloat16),
                        pltpu.VMEM((orb, blk), jnp.bfloat16),
                        dma((4,)), dma((groups, 2, rows)), dma((groups, 2, rows)),
                        dma((groups, 2)), dma((groups, 2)), dma, dma, dma((groups,)), dma((groups,))],
        compiler_params=pltpu.CompilerParams(collective_id=0, has_side_effects=True, vmem_limit_bytes=40 << 20),
    )(final_amp[0], initial_amp[0], map_final[0][:, None], map_initial[0][:, None], lists)
    i_all = i_all.reshape(-1, orb, blk)
    unit = 8 * rows * cols
    total = pl.cdiv(pl.cdiv(orb, LANES) * orb, unit) * unit
    partial = pl.pallas_call(
        functools.partial(density_kernel, rows, cols, own_f, own_i),
        out_shape=jax.ShapeDtypeStruct((total, LANES), jnp.float32),
        in_specs=[vmem, vmem, pl.BlockSpec(memory_space=pltpu.SMEM)],
        out_specs=vmem,
        scratch_shapes=[pltpu.VMEM((orb, orb), jnp.float32)]
        + [pltpu.SMEM((groups * slots + UNROLL,), jnp.int32)] * 2,
        compiler_params=pltpu.CompilerParams(vmem_limit_bytes=50 << 20),
    )(f_all, i_all, l_all)
    size = total // 2 // rows
    steps = rows.bit_length() - 1
    return pl.pallas_call(
        functools.partial(reduce_kernel, rows, cols),
        out_shape=jax.ShapeDtypeStruct((orb, orb), jnp.float32),
        in_specs=[vmem],
        out_specs=vmem,
        scratch_shapes=[pltpu.VMEM((total, LANES), jnp.float32), pltpu.VMEM((total, LANES), jnp.float32),
                        pltpu.VMEM((2, total // 2, LANES), jnp.float32),
                        pltpu.VMEM((cols - 1, size // (cols // 2), LANES), jnp.float32),
                        dma((2, steps)), dma((2, steps)), dma((cols,)), dma((cols,)), dma((cols,)), dma((cols,)),
                        dma((2, steps)), dma((2, steps))],
        compiler_params=pltpu.CompilerParams(collective_id=1, has_side_effects=True, vmem_limit_bytes=40 << 20),
    )(partial)


def solution(mesh):
    placed = (
        P("row", "col", None, None),
        P("col", "row", None, None),
        P("row", "col", None),
        P("row", "col", None),
        P("row", "col", None),
        P("col", "row", None),
        P("row", "col"),
    )
    body = functools.partial(shards, mesh.shape["row"], mesh.shape["col"])
    return jax.shard_map(body, mesh=mesh, in_specs=placed, out_specs=P(), check_vma=False)
```

```python
import functools

import jax
import jax.numpy as jnp
from jax import lax
from jax.experimental import pallas as pl
from jax.experimental.pallas import tpu as pltpu
from jax.sharding import PartitionSpec as P

MESH = pl.DeviceIdType.MESH
UNROLL = 8
CHUNKS = 3
LANES = 128


def flip(value, bit):
    return value + bit - 2 * bit * lax.rem(lax.div(value, bit), 2)


def flip_many(value, mask):
    bit = 1
    while bit <= mask:
        if mask & bit:
            value = flip(value, bit)
        bit *= 2
    return value


def relay_plan(rows):
    bits = []
    bit = 2
    while bit < rows:
        bits.append(bit)
        bit *= 2
    plans = []
    for order in (bits, bits[::-1]):
        diffs = [(0, 0)]
        for position, bit in enumerate(order):
            diffs += [(diff | bit, position + 1) for diff, _ in list(diffs)]
        plans.append((order, diffs))
    return plans


def permute(block, stored):
    orbitals = block.shape[0]
    chosen = lax.broadcasted_iota(jnp.int32, (orbitals, orbitals), 1) == stored
    onehot = jnp.where(chosen, 1.0, 0.0).astype(jnp.bfloat16)
    return jnp.dot(onehot, block, preferred_element_type=jnp.float32).astype(jnp.bfloat16)


def spread_kernel(rows, cols, fin_ref, ini_ref, fmap_ref, imap_ref, pf_ref, pi_ref, count_ref, f_all, i_all, l_all,
                  list_ref, f_own, i_own, zero, local_sem, send_sem, recv_sem, zsend, zrecv, fsend, frecv, lsend, lrecv):
    r = lax.axis_index("row")
    c = lax.axis_index("col")
    groups = cols // 2
    own_i = ini_ref.shape[1]
    own_f = fin_ref.shape[1]
    half = own_i // 2
    plans = relay_plan(rows)

    barrier = pltpu.get_barrier_semaphore()
    peers = []
    bit = 1
    while bit < rows:
        peers.append((flip(r, bit), c))
        bit *= 2
    peers += [(r, flip_many(c, mask)) for mask in [1] + [2 * g for g in range(1, groups)]]
    for peer in peers:
        pl.semaphore_signal(barrier, inc=1, device_id=peer, device_id_type=MESH)

    list_ref[0:1] = pf_ref[0]
    list_ref[1:2] = pi_ref[0]
    list_ref[2:8] = jnp.full((6, list_ref.shape[1]), count_ref[0, 0], jnp.int32)
    stored = imap_ref[0].T
    for j in range(own_i):
        i_own[j] = permute(ini_ref[0, j], stored[:, j:j + 1])
    pl.semaphore_wait(barrier, len(peers))

    sent = []

    def remote(src, dst, ssem, rsem, peer):
        copy = pltpu.make_async_remote_copy(src_ref=src, dst_ref=dst, send_sem=ssem, recv_sem=rsem,
                                            device_id=peer, device_id_type=MESH)
        copy.start()
        sent.append(copy)

    def part(h):
        return pl.ds(h * half, half)

    used = {}

    def forward(g, h, diff, position, src):
        order, _ = plans[h]
        targets = order[position:] + [1]
        for bit in targets:
            k = used.setdefault((g, h), 0)
            used[(g, h)] = k + 1
            remote(src, i_all.at[g, diff ^ bit, part(h)], send_sem.at[g, h, k], recv_sem.at[g, h, diff ^ bit],
                   (flip(r, bit), c))

    for h in range(2):
        for g in range(1, groups):
            remote(i_own.at[part(h)], i_all.at[g, 0, part(h)], zsend.at[g, h], zrecv.at[g, h], (r, flip_many(c, 2 * g)))
        forward(0, h, 0, 0, i_own.at[part(h)])
    for g in range(1, groups):
        remote(list_ref, l_all.at[g], lsend.at[g], lrecv.at[g], (r, flip_many(c, 2 * g)))

    local = [pltpu.make_async_copy(i_own, i_all.at[0, 0], local_sem.at[0]),
             pltpu.make_async_copy(list_ref, l_all.at[0], local_sem.at[1])]
    zero[...] = jnp.zeros_like(zero)
    stored = fmap_ref[0].T
    for j in range(own_f):
        f_own[j] = permute(fin_ref[0, j], stored[:, j:j + 1])
    remote(f_own, f_all.at[pl.ds(own_f, own_f)], fsend, frecv, (r, flip(c, 1)))
    local += [pltpu.make_async_copy(f_own, f_all.at[pl.ds(0, own_f)], local_sem.at[2]),
              pltpu.make_async_copy(zero, f_all.at[2 * own_f], local_sem.at[3])]
    for copy in local:
        copy.start()

    def arrived(ref, ssem, rsem):
        pltpu.make_async_remote_copy(src_ref=ref, dst_ref=ref, send_sem=ssem, recv_sem=rsem,
                                     device_id=(flip(r, 1), c), device_id_type=MESH).wait_recv()

    def relay(g, h, diff, position):
        here = i_all.at[g, diff, part(h)]
        if diff == 0:
            arrived(here, zsend.at[g, h], zrecv.at[g, h])
        else:
            arrived(here, send_sem.at[g, h, 0], recv_sem.at[g, h, diff])
        forward(g, h, diff, position, here)

    longest = len(plans[0][1])
    for wave in range(groups + longest):
        for g in range(groups):
            index = wave - g + 1
            if g == 0 and index == 0:
                continue
            for h in range(2):
                if g > 0:
                    index = wave - g
                if 0 <= index < longest:
                    diff, position = plans[h][1][index]
                    if g == 0 and diff == 0:
                        continue
                    relay(g, h, diff, position)
    for g in range(groups):
        for h in range(2):
            for diff, _ in plans[h][1]:
                arrived(i_all.at[g, diff ^ 1, part(h)], send_sem.at[g, h, 0], recv_sem.at[g, h, diff ^ 1])
    for g in range(1, groups):
        arrived(l_all.at[g], lsend.at[g], lrecv.at[g])
    arrived(f_all.at[pl.ds(own_f, own_f)], fsend, frecv)
    for copy in sent:
        copy.wait_send()
    for copy in local:
        copy.wait()


def density_kernel(rows, cols, own_f, own_i, f_ref, i_ref, l_ref, out_ref, acc, list_f, list_i):
    r = lax.axis_index("row")
    c = lax.axis_index("col")
    groups = cols // 2
    total = jnp.int32(0)
    for g in range(groups):
        def collect(p, n):
            q = l_ref[g, 0, p]
            s = l_ref[g, 1, p]
            apart = lax.div(q, own_f) ^ c
            list_f[n] = apart * own_f + lax.rem(q, own_f)
            list_i[n] = (g * rows + (lax.div(s, own_i) ^ r)) * own_i + lax.rem(s, own_i)
            return n + jnp.where(apart < 2, 1, 0).astype(jnp.int32)

        total = lax.fori_loop(0, l_ref[g, 2, 0], collect, total)
    for k in range(UNROLL):
        list_f[total + k] = 2 * own_f
        list_i[total + k] = 0
    acc[...] = jnp.zeros_like(acc)

    def step(t, carry):
        first = t * UNROLL
        left = jnp.concatenate([f_ref[list_f[first + k]] for k in range(UNROLL)], axis=1)
        right = jnp.concatenate([i_ref[list_i[first + k]] for k in range(UNROLL)], axis=1)
        acc[...] += lax.dot_general(left, right, (((1,), (1,)), ((), ())), preferred_element_type=jnp.float32)
        return carry

    lax.fori_loop(0, lax.div(total + UNROLL - 1, UNROLL), step, 0)
    orb = acc.shape[0]
    for block, first in enumerate(range(0, orb, LANES)):
        width = min(LANES, orb - first)
        if width < LANES:
            out_ref[block * orb:, :] = jnp.zeros((out_ref.shape[0] - block * orb, LANES), jnp.float32)
        out_ref[block * orb:(block + 1) * orb, :width] = acc[:, first:first + width]
    tail = pl.cdiv(orb, LANES) * orb
    if tail < out_ref.shape[0]:
        out_ref[tail:, :] = jnp.zeros((out_ref.shape[0] - tail, LANES), jnp.float32)


def chunks(total, unit):
    units = total // unit
    count = min(CHUNKS, units)
    pieces = []
    base = 0
    for n in range(count):
        length = (units // count + (n < units % count)) * unit
        pieces.append((base, length))
        base += length
    return pieces


def reduce_kernel(rows, cols, part_ref, out_ref, acc, res, rbuf, zbuf,
                  rs_send, rs_recv, z_send, z_recv, g_send, g_recv, ag_send, ag_recv):
    r = lax.axis_index("row")
    c = lax.axis_index("col")
    orders = [[1] + order for order, _ in relay_plan(rows)]
    steps = len(orders[0])

    barrier = pltpu.get_barrier_semaphore()
    peers = [(flip(r, bit), c) for bit in orders[0]] + [(r, flip_many(c, mask)) for mask in range(1, cols)]
    for peer in peers:
        pl.semaphore_signal(barrier, inc=1, device_id=peer, device_id_type=MESH)
    pl.semaphore_wait(barrier, len(peers))

    sent = []

    def remote(src, dst, ssem, rsem, peer):
        copy = pltpu.make_async_remote_copy(src_ref=src, dst_ref=dst, send_sem=ssem, recv_sem=rsem,
                                            device_id=peer, device_id_type=MESH)
        copy.start()
        sent.append(copy)
        return copy

    def rows_at(first, size):
        return pl.ds(pl.multiple_of(first, 8), size)

    share = cols // 2

    def chain(n, base, length):
        half = length // 2
        start = [r * 0 + base, r * 0 + base + half]
        size = half
        used = base // 2
        for step in range(steps):
            size //= 2
            source = part_ref if step == 0 else acc
            copies = []
            for h in range(2):
                bit = orders[h][step]
                mine = lax.rem(lax.div(r, bit), 2)
                give = start[h] + (1 - mine) * size
                start[h] = start[h] + mine * size
                copies.append(remote(source.at[rows_at(give, size)], rbuf.at[h, pl.ds(used, size)],
                                     rs_send.at[n, h, step], rs_recv.at[n, h, step], (flip(r, bit), c)))
            yield
            for h in range(2):
                copies[h].wait_recv()
                keep = rows_at(start[h], size)
                acc[keep, :] = source[keep, :] + rbuf[h, used:used + size, :]
            used += size
        sub = size // share

        def band(k):
            return rows_at(start[0] + (start[1] - start[0]) * lax.div(k, share) + lax.rem(k, share) * sub, sub)

        own = band(c)
        copies = []
        for mask in range(1, cols):
            peer = flip_many(c, mask)
            copies.append(remote(acc.at[band(peer)], zbuf.at[n, mask - 1, pl.ds(0, sub)],
                                 z_send.at[n, mask], z_recv.at[n, mask], (r, peer)))
        yield
        value = acc[own, :]
        for mask in range(1, cols):
            copies[mask - 1].wait_recv()
            value = value + zbuf[n, mask - 1, :sub]
        res[own, :] = value
        copies = []
        for mask in range(1, cols):
            copies.append(remote(res.at[own], res.at[own], g_send.at[n, mask], g_recv.at[n, mask],
                                 (r, flip_many(c, mask))))
        yield
        for copy in copies:
            copy.wait_recv()
        for step in reversed(range(steps)):
            copies = []
            for h in range(2):
                bit = orders[h][step]
                here = res.at[rows_at(start[h], size)]
                copies.append(remote(here, here, ag_send.at[n, h, step], ag_recv.at[n, h, step], (flip(r, bit), c)))
            yield
            for h in range(2):
                copies[h].wait_recv()
                start[h] = start[h] - lax.rem(lax.div(r, orders[h][step]), 2) * size
            size *= 2

    chains = [chain(n, *piece) for n, piece in enumerate(chunks(part_ref.shape[0], 8 * rows * cols))]
    while chains:
        for link in list(chains):
            try:
                next(link)
            except StopIteration:
                chains.remove(link)
    orb = out_ref.shape[0]
    for block, first in enumerate(range(0, orb, LANES)):
        width = min(LANES, orb - first)
        out_ref[:, first:first + width] = res[block * orb:(block + 1) * orb, :width]
    for copy in sent:
        copy.wait_send()


def shards(rows, cols, final_amp, initial_amp, pair_final, pair_initial, map_final, map_initial, counts):
    own_f, blk, orb = final_amp.shape[1:]
    own_i = initial_amp.shape[1]
    slots = pair_final.shape[2]
    groups = cols // 2
    vmem = pl.BlockSpec(memory_space=pltpu.VMEM)
    hbm = pl.BlockSpec(memory_space=pl.ANY)
    dma = pltpu.SemaphoreType.DMA
    f_all, i_all, l_all = pl.pallas_call(
        functools.partial(spread_kernel, rows, cols),
        out_shape=(jax.ShapeDtypeStruct((2 * own_f + 1, orb, blk), jnp.bfloat16),
                   jax.ShapeDtypeStruct((groups, rows, own_i, orb, blk), jnp.bfloat16),
                   jax.ShapeDtypeStruct((groups, 8, slots), jnp.int32)),
        in_specs=[vmem] * 6 + [pl.BlockSpec(memory_space=pltpu.SMEM)],
        out_specs=(hbm, hbm, hbm),
        scratch_shapes=[pltpu.VMEM((8, slots), jnp.int32), pltpu.VMEM((own_f, orb, blk), jnp.bfloat16), pltpu.VMEM((own_i, orb, blk), jnp.bfloat16),
                        pltpu.VMEM((orb, blk), jnp.bfloat16),
                        dma((4,)), dma((groups, 2, rows)), dma((groups, 2, rows)),
                        dma((groups, 2)), dma((groups, 2)), dma, dma, dma((groups,)), dma((groups,))],
        compiler_params=pltpu.CompilerParams(collective_id=0, has_side_effects=True, vmem_limit_bytes=20 << 20),
    )(final_amp.swapaxes(2, 3), initial_amp.swapaxes(2, 3), map_final, map_initial, pair_final, pair_initial, counts)
    i_all = i_all.reshape(-1, orb, blk)
    unit = 8 * rows * cols
    total = pl.cdiv(pl.cdiv(orb, LANES) * orb, unit) * unit
    partial = pl.pallas_call(
        functools.partial(density_kernel, rows, cols, own_f, own_i),
        out_shape=jax.ShapeDtypeStruct((total, LANES), jnp.float32),
        in_specs=[vmem, vmem, pl.BlockSpec(memory_space=pltpu.SMEM)],
        out_specs=vmem,
        scratch_shapes=[pltpu.VMEM((orb, orb), jnp.float32)]
        + [pltpu.SMEM((groups * slots + UNROLL,), jnp.int32)] * 2,
        compiler_params=pltpu.CompilerParams(vmem_limit_bytes=20 << 20),
    )(f_all, i_all, l_all)
    pieces = chunks(total, unit)
    many = len(pieces)
    largest = pieces[0][1] // 2 // rows // (cols // 2)
    steps = rows.bit_length() - 1
    return pl.pallas_call(
        functools.partial(reduce_kernel, rows, cols),
        out_shape=jax.ShapeDtypeStruct((orb, orb), jnp.float32),
        in_specs=[vmem],
        out_specs=vmem,
        scratch_shapes=[pltpu.VMEM((total, LANES), jnp.float32), pltpu.VMEM((total, LANES), jnp.float32),
                        pltpu.VMEM((2, total // 2, LANES), jnp.float32),
                        pltpu.VMEM((many, cols - 1, largest, LANES), jnp.float32),
                        dma((many, 2, steps)), dma((many, 2, steps)), dma((many, cols)), dma((many, cols)),
                        dma((many, cols)), dma((many, cols)), dma((many, 2, steps)), dma((many, 2, steps))],
        compiler_params=pltpu.CompilerParams(collective_id=1, has_side_effects=True, vmem_limit_bytes=20 << 20),
    )(partial)


def solution(mesh):
    placed = (
        P("row", "col", None, None),
        P("col", "row", None, None),
        P("row", "col", None),
        P("row", "col", None),
        P("row", "col", None),
        P("col", "row", None),
        P("row", "col"),
    )
    body = functools.partial(shards, mesh.shape["row"], mesh.shape["col"])
    return jax.shard_map(body, mesh=mesh, in_specs=placed, out_specs=P(), check_vma=False)
```

```python
import functools

import jax
import jax.numpy as jnp
from jax import lax
from jax.experimental import pallas as pl
from jax.experimental.pallas import tpu as pltpu
from jax.sharding import PartitionSpec as P

MESH = pl.DeviceIdType.MESH
UNROLL = 8
CHUNKS = 4
LANES = 128


def flip(value, bit):
    return value + bit - 2 * bit * lax.rem(lax.div(value, bit), 2)


def flip_many(value, mask):
    bit = 1
    while bit <= mask:
        if mask & bit:
            value = flip(value, bit)
        bit *= 2
    return value


def relay_plan(rows):
    bits = []
    bit = 2
    while bit < rows:
        bits.append(bit)
        bit *= 2
    plans = []
    for order in (bits, bits[::-1]):
        diffs = [(0, 0)]
        for position, bit in enumerate(order):
            diffs += [(diff | bit, position + 1) for diff, _ in list(diffs)]
        plans.append((order, diffs))
    return plans


def permute(block, stored):
    orbitals = block.shape[0]
    chosen = lax.broadcasted_iota(jnp.int32, (orbitals, orbitals), 1) == stored
    onehot = jnp.where(chosen, 1.0, 0.0).astype(jnp.bfloat16)
    return jnp.dot(onehot, block, preferred_element_type=jnp.float32).astype(jnp.bfloat16)


def spread_kernel(rows, cols, fin_hbm, ini_hbm, fmap_hbm, imap_hbm, pf_hbm, pi_hbm, count_ref, f_all, i_all, l_all,
                  fin_ref, ini_ref, fmap_ref, imap_ref, pf_ref, pi_ref, load_sem, list_ref, f_own, i_own, zero, local_sem, send_sem, recv_sem, zsend, zrecv, fsend, frecv, lsend, lrecv):
    r = lax.axis_index("row")
    c = lax.axis_index("col")
    groups = cols // 2
    pairs = ((imap_hbm, imap_ref), (ini_hbm, ini_ref), (pf_hbm, pf_ref), (pi_hbm, pi_ref),
             (fmap_hbm, fmap_ref), (fin_hbm, fin_ref))
    loads = [pltpu.make_async_copy(src, dst, load_sem.at[n]) for n, (src, dst) in enumerate(pairs)]
    for load in loads:
        load.start()
    own_i = ini_ref.shape[1]
    own_f = fin_ref.shape[1]
    half = own_i // 2
    plans = relay_plan(rows)

    barrier = pltpu.get_barrier_semaphore()
    peers = []
    bit = 1
    while bit < rows:
        peers.append((flip(r, bit), c))
        bit *= 2
    peers += [(r, flip_many(c, mask)) for mask in [1] + [2 * g for g in range(1, groups)]]
    for peer in peers:
        pl.semaphore_signal(barrier, inc=1, device_id=peer, device_id_type=MESH)

    for load in loads[:4]:
        load.wait()
    list_ref[0:1] = pf_ref[0]
    list_ref[1:2] = pi_ref[0]
    list_ref[2:8] = jnp.full((6, list_ref.shape[1]), count_ref[0, 0], jnp.int32)
    stored = imap_ref[0].T
    for j in range(own_i):
        i_own[j] = permute(ini_ref[0, j], stored[:, j:j + 1])
    pl.semaphore_wait(barrier, len(peers))

    sent = []

    def remote(src, dst, ssem, rsem, peer):
        copy = pltpu.make_async_remote_copy(src_ref=src, dst_ref=dst, send_sem=ssem, recv_sem=rsem,
                                            device_id=peer, device_id_type=MESH)
        copy.start()
        sent.append(copy)

    def part(h):
        return pl.ds(h * half, half)

    used = {}

    def forward(g, h, diff, position, src):
        order, _ = plans[h]
        targets = order[position:] + [1]
        for bit in targets:
            k = used.setdefault((g, h), 0)
            used[(g, h)] = k + 1
            remote(src, i_all.at[g, diff ^ bit, part(h)], send_sem.at[g, h, k], recv_sem.at[g, h, diff ^ bit],
                   (flip(r, bit), c))

    for h in range(2):
        for g in range(1, groups):
            remote(i_own.at[part(h)], i_all.at[g, 0, part(h)], zsend.at[g, h], zrecv.at[g, h], (r, flip_many(c, 2 * g)))
        forward(0, h, 0, 0, i_own.at[part(h)])
    for g in range(1, groups):
        remote(list_ref, l_all.at[g], lsend.at[g], lrecv.at[g], (r, flip_many(c, 2 * g)))

    local = [pltpu.make_async_copy(i_own, i_all.at[0, 0], local_sem.at[0]),
             pltpu.make_async_copy(list_ref, l_all.at[0], local_sem.at[1])]
    zero[...] = jnp.zeros_like(zero)
    for load in loads[4:]:
        load.wait()
    stored = fmap_ref[0].T
    for j in range(own_f):
        f_own[j] = permute(fin_ref[0, j], stored[:, j:j + 1])
    remote(f_own, f_all.at[pl.ds(own_f, own_f)], fsend, frecv, (r, flip(c, 1)))
    local += [pltpu.make_async_copy(f_own, f_all.at[pl.ds(0, own_f)], local_sem.at[2]),
              pltpu.make_async_copy(zero, f_all.at[2 * own_f], local_sem.at[3])]
    for copy in local:
        copy.start()

    def arrived(ref, ssem, rsem):
        pltpu.make_async_remote_copy(src_ref=ref, dst_ref=ref, send_sem=ssem, recv_sem=rsem,
                                     device_id=(flip(r, 1), c), device_id_type=MESH).wait_recv()

    def relay(g, h, diff, position):
        here = i_all.at[g, diff, part(h)]
        if diff == 0:
            arrived(here, zsend.at[g, h], zrecv.at[g, h])
        else:
            arrived(here, send_sem.at[g, h, 0], recv_sem.at[g, h, diff])
        forward(g, h, diff, position, here)

    longest = len(plans[0][1])
    for wave in range(groups + longest):
        for g in range(groups):
            index = wave - g + 1
            if g == 0 and index == 0:
                continue
            for h in range(2):
                if g > 0:
                    index = wave - g
                if 0 <= index < longest:
                    diff, position = plans[h][1][index]
                    if g == 0 and diff == 0:
                        continue
                    relay(g, h, diff, position)
    for g in range(groups):
        for h in range(2):
            for diff, _ in plans[h][1]:
                arrived(i_all.at[g, diff ^ 1, part(h)], send_sem.at[g, h, 0], recv_sem.at[g, h, diff ^ 1])
    for g in range(1, groups):
        arrived(l_all.at[g], lsend.at[g], lrecv.at[g])
    arrived(f_all.at[pl.ds(own_f, own_f)], fsend, frecv)
    for copy in sent:
        copy.wait_send()
    for copy in local:
        copy.wait()


def density_kernel(rows, cols, own_f, own_i, f_hbm, i_hbm, l_ref, out_ref, f_ref, i_ref, load_sem, acc, list_f, list_i):
    loads = [pltpu.make_async_copy(i_hbm, i_ref, load_sem.at[0]), pltpu.make_async_copy(f_hbm, f_ref, load_sem.at[1])]
    for load in loads:
        load.start()
    r = lax.axis_index("row")
    c = lax.axis_index("col")
    groups = cols // 2
    total = jnp.int32(0)
    for g in range(groups):
        def collect(p, n):
            q = l_ref[g, 0, p]
            s = l_ref[g, 1, p]
            apart = lax.div(q, own_f) ^ c
            list_f[n] = apart * own_f + lax.rem(q, own_f)
            list_i[n] = (g * rows + (lax.div(s, own_i) ^ r)) * own_i + lax.rem(s, own_i)
            return n + jnp.where(apart < 2, 1, 0).astype(jnp.int32)

        total = lax.fori_loop(0, l_ref[g, 2, 0], collect, total)
    for k in range(UNROLL):
        list_f[total + k] = 2 * own_f
        list_i[total + k] = 0
    acc[...] = jnp.zeros_like(acc)
    for load in loads:
        load.wait()

    def step(t, carry):
        first = t * UNROLL
        left = jnp.concatenate([f_ref[list_f[first + k]] for k in range(UNROLL)], axis=1)
        right = jnp.concatenate([i_ref[list_i[first + k]] for k in range(UNROLL)], axis=1)
        acc[...] += lax.dot_general(left, right, (((1,), (1,)), ((), ())), preferred_element_type=jnp.float32)
        return carry

    lax.fori_loop(0, lax.div(total + UNROLL - 1, UNROLL), step, 0)
    orb = acc.shape[0]
    for block, first in enumerate(range(0, orb, LANES)):
        width = min(LANES, orb - first)
        if width < LANES:
            out_ref[block * orb:, :] = jnp.zeros((out_ref.shape[0] - block * orb, LANES), jnp.float32)
        out_ref[block * orb:(block + 1) * orb, :width] = acc[:, first:first + width]
    tail = pl.cdiv(orb, LANES) * orb
    if tail < out_ref.shape[0]:
        out_ref[tail:, :] = jnp.zeros((out_ref.shape[0] - tail, LANES), jnp.float32)


def chunks(total, unit):
    units = total // unit
    count = min(CHUNKS, units)
    pieces = []
    base = 0
    for n in range(count):
        length = (units // count + (n < units % count)) * unit
        pieces.append((base, length))
        base += length
    return pieces


def reduce_kernel(rows, cols, part_ref, out_ref, acc, res, rbuf, zbuf,
                  rs_send, rs_recv, z_send, z_recv, g_send, g_recv, ag_send, ag_recv):
    r = lax.axis_index("row")
    c = lax.axis_index("col")
    orders = [[1] + order for order, _ in relay_plan(rows)]
    steps = len(orders[0])

    barrier = pltpu.get_barrier_semaphore()
    peers = [(flip(r, bit), c) for bit in orders[0]] + [(r, flip_many(c, mask)) for mask in range(1, cols)]
    for peer in peers:
        pl.semaphore_signal(barrier, inc=1, device_id=peer, device_id_type=MESH)
    pl.semaphore_wait(barrier, len(peers))

    sent = []

    def remote(src, dst, ssem, rsem, peer):
        copy = pltpu.make_async_remote_copy(src_ref=src, dst_ref=dst, send_sem=ssem, recv_sem=rsem,
                                            device_id=peer, device_id_type=MESH)
        copy.start()
        sent.append(copy)
        return copy

    def rows_at(first, size):
        return pl.ds(pl.multiple_of(first, 8), size)

    share = cols // 2

    def chain(n, base, length):
        half = length // 2
        start = [r * 0 + base, r * 0 + base + half]
        size = half
        used = base // 2
        for step in range(steps):
            size //= 2
            source = part_ref if step == 0 else acc
            copies = []
            for h in range(2):
                bit = orders[h][step]
                mine = lax.rem(lax.div(r, bit), 2)
                give = start[h] + (1 - mine) * size
                start[h] = start[h] + mine * size
                copies.append(remote(source.at[rows_at(give, size)], rbuf.at[h, pl.ds(used, size)],
                                     rs_send.at[n, h, step], rs_recv.at[n, h, step], (flip(r, bit), c)))
            yield
            for h in range(2):
                copies[h].wait_recv()
                keep = rows_at(start[h], size)
                acc[keep, :] = source[keep, :] + rbuf[h, used:used + size, :]
            used += size
        sub = size // share

        def band(k):
            return rows_at(start[0] + (start[1] - start[0]) * lax.div(k, share) + lax.rem(k, share) * sub, sub)

        own = band(c)
        copies = []
        for mask in range(1, cols):
            peer = flip_many(c, mask)
            copies.append(remote(acc.at[band(peer)], zbuf.at[n, mask - 1, pl.ds(0, sub)],
                                 z_send.at[n, mask], z_recv.at[n, mask], (r, peer)))
        yield
        value = acc[own, :]
        for mask in range(1, cols):
            copies[mask - 1].wait_recv()
            value = value + zbuf[n, mask - 1, :sub]
        res[own, :] = value
        copies = []
        for mask in range(1, cols):
            copies.append(remote(res.at[own], res.at[own], g_send.at[n, mask], g_recv.at[n, mask],
                                 (r, flip_many(c, mask))))
        yield
        for copy in copies:
            copy.wait_recv()
        for step in reversed(range(steps)):
            copies = []
            for h in range(2):
                bit = orders[h][step]
                here = res.at[rows_at(start[h], size)]
                copies.append(remote(here, here, ag_send.at[n, h, step], ag_recv.at[n, h, step], (flip(r, bit), c)))
            yield
            for h in range(2):
                copies[h].wait_recv()
                start[h] = start[h] - lax.rem(lax.div(r, orders[h][step]), 2) * size
            size *= 2

    chains = [chain(n, *piece) for n, piece in enumerate(chunks(part_ref.shape[0], 8 * rows * cols))]
    while chains:
        for link in list(chains):
            try:
                next(link)
            except StopIteration:
                chains.remove(link)
    orb = out_ref.shape[0]
    for block, first in enumerate(range(0, orb, LANES)):
        width = min(LANES, orb - first)
        out_ref[:, first:first + width] = res[block * orb:(block + 1) * orb, :width]
    for copy in sent:
        copy.wait_send()


def shards(rows, cols, final_amp, initial_amp, pair_final, pair_initial, map_final, map_initial, counts):
    own_f, blk, orb = final_amp.shape[1:]
    own_i = initial_amp.shape[1]
    slots = pair_final.shape[2]
    groups = cols // 2
    vmem = pl.BlockSpec(memory_space=pltpu.VMEM)
    hbm = pl.BlockSpec(memory_space=pl.ANY)
    dma = pltpu.SemaphoreType.DMA
    f_all, i_all, l_all = pl.pallas_call(
        functools.partial(spread_kernel, rows, cols),
        out_shape=(jax.ShapeDtypeStruct((2 * own_f + 1, orb, blk), jnp.bfloat16),
                   jax.ShapeDtypeStruct((groups, rows, own_i, orb, blk), jnp.bfloat16),
                   jax.ShapeDtypeStruct((groups, 8, slots), jnp.int32)),
        in_specs=[pl.BlockSpec(memory_space=pltpu.HBM)] * 6 + [pl.BlockSpec(memory_space=pltpu.SMEM)],
        out_specs=(hbm, hbm, hbm),
        scratch_shapes=[pltpu.VMEM((1, own_f, orb, blk), jnp.bfloat16), pltpu.VMEM((1, own_i, orb, blk), jnp.bfloat16),
                        pltpu.VMEM(map_final.shape, jnp.int32), pltpu.VMEM(map_initial.shape, jnp.int32),
                        pltpu.VMEM(pair_final.shape, jnp.int32), pltpu.VMEM(pair_initial.shape, jnp.int32),
                        dma((6,)), pltpu.VMEM((8, slots), jnp.int32), pltpu.VMEM((own_f, orb, blk), jnp.bfloat16), pltpu.VMEM((own_i, orb, blk), jnp.bfloat16),
                        pltpu.VMEM((orb, blk), jnp.bfloat16),
                        dma((4,)), dma((groups, 2, rows)), dma((groups, 2, rows)),
                        dma((groups, 2)), dma((groups, 2)), dma, dma, dma((groups,)), dma((groups,))],
        compiler_params=pltpu.CompilerParams(collective_id=0, has_side_effects=True, vmem_limit_bytes=56 << 20),
    )(final_amp.swapaxes(2, 3), initial_amp.swapaxes(2, 3), map_final, map_initial, pair_final, pair_initial, counts)
    i_all = i_all.reshape(-1, orb, blk)
    unit = 8 * rows * cols
    total = pl.cdiv(pl.cdiv(orb, LANES) * orb, unit) * unit
    partial = pl.pallas_call(
        functools.partial(density_kernel, rows, cols, own_f, own_i),
        out_shape=jax.ShapeDtypeStruct((total, LANES), jnp.float32),
        in_specs=[pl.BlockSpec(memory_space=pltpu.HBM)] * 2 + [pl.BlockSpec(memory_space=pltpu.SMEM)],
        out_specs=vmem,
        scratch_shapes=[pltpu.VMEM(f_all.shape, jnp.bfloat16), pltpu.VMEM(i_all.shape, jnp.bfloat16), dma((2,)),
                        pltpu.VMEM((orb, orb), jnp.float32)]
        + [pltpu.SMEM((groups * slots + UNROLL,), jnp.int32)] * 2,
        compiler_params=pltpu.CompilerParams(vmem_limit_bytes=56 << 20),
    )(f_all, i_all, l_all)
    pieces = chunks(total, unit)
    many = len(pieces)
    largest = pieces[0][1] // 2 // rows // (cols // 2)
    steps = rows.bit_length() - 1
    return pl.pallas_call(
        functools.partial(reduce_kernel, rows, cols),
        out_shape=jax.ShapeDtypeStruct((orb, orb), jnp.float32),
        in_specs=[vmem],
        out_specs=vmem,
        scratch_shapes=[pltpu.VMEM((total, LANES), jnp.float32), pltpu.VMEM((total, LANES), jnp.float32),
                        pltpu.VMEM((2, total // 2, LANES), jnp.float32),
                        pltpu.VMEM((many, cols - 1, largest, LANES), jnp.float32),
                        dma((many, 2, steps)), dma((many, 2, steps)), dma((many, cols)), dma((many, cols)),
                        dma((many, cols)), dma((many, cols)), dma((many, 2, steps)), dma((many, 2, steps))],
        compiler_params=pltpu.CompilerParams(collective_id=1, has_side_effects=True, vmem_limit_bytes=20 << 20),
    )(partial)


def solution(mesh):
    placed = (
        P("row", "col", None, None),
        P("col", "row", None, None),
        P("row", "col", None),
        P("row", "col", None),
        P("row", "col", None),
        P("col", "row", None),
        P("row", "col"),
    )
    body = functools.partial(shards, mesh.shape["row"], mesh.shape["col"])
    return jax.shard_map(body, mesh=mesh, in_specs=placed, out_specs=P(), check_vma=False)
```
